32 devices in a mesh: sect: 2 (over core), tok: 2 (over x), vocab: 8 (over z, y).
Axes of the slice: x: 2, y: 2, z: 4, core: 2. Of those that a mesh axis runs over, the one named last changes fastest.
Arguments:
- teacher_hidden: bfloat16 [512, 8192], P('tok', 'sect'), may hold values from -6 to 6
- teacher_head: bfloat16 [8192, 4096], P('sect', 'vocab'), may hold values from -0.19921875 to 0.19921875
- student_hidden: bfloat16 [512, 3072], P('tok', 'sect'), may hold values from -6 to 6
- student_head: bfloat16 [3072, 4096], P('sect', 'vocab'), may hold values from -0.328125 to 0.328125
- live_counts: int32 [2], P('tok'), may hold values from 1 to 256, 384 in all
Outputs:
- loss: float32 [], replicated
- head_grad: bfloat16 [3072, 4096], P(('sect', 'tok'), 'vocab')
- hidden_grad: bfloat16 [512, 3072], P(('tok', 'vocab'), 'sect')
The draws below stay inside these ranges and needn't reach their ends.
Inputs may be any that keep to these rules, and one draw needn't show every extreme that they name: Shard k of the tokens has its first live_counts[k] token slots live and the rest empty.
All inputs are finite; a program needn't handle non-finite values.
Results may differ from the reference program's by a relative error of at most 0.0049.
Values may be sent and summed in bfloat16 or wider, within the bound.
A program may use at most 64 MiB of HBM per device.

```python
import math
import jax
import jax.numpy as jnp
import numpy as np

DT = 8192
DS = 3072
TOK_DEV = 256
VOCAB = 4096
TOKENS = 512
N_TOK = 2


def block_levels(rng, dims, shards, low, largest):
    factor_of, own = 1.0, jax.random.fold_in(rng, 6)
    for dim, blocks in shards:
        draws = jnp.exp(jax.random.uniform(jax.random.fold_in(own, dim), (blocks,), jnp.float32, low / len(shards), largest / len(shards)))
        factor_of = factor_of * jnp.repeat(draws, dims[dim] // blocks).reshape([-1 if axis == dim else 1 for axis in range(len(dims))])
    return factor_of


def split_up(number_of, total, bound, lean):
    loads = [(1 << 20) // math.isqrt(grade ** lean) + 1 for grade in range(2, number_of + 1)]
    rest, counts = total - bound - (number_of - 1), [1] * (number_of - 1)
    while rest > 0:
        free = [i for i in range(number_of - 1) if counts[i] < bound]
        pool, remaining = sum([loads[i] for i in free]), rest
        for i in free:
            more = min(bound - counts[i], max(1, remaining * loads[i] // pool), rest)
            counts[i] = counts[i] + more
            rest = rest - more
    return np.array([bound] + counts)


def uneven_parts(key, amount, total, bound, slope):
    if amount == 2:
        one = jax.random.randint(key, (), max(1, total - bound), min(bound, total - 1) + 1)
        return jnp.stack([one, total - one])
    sizes = jnp.asarray(split_up(amount, total, bound, slope), jnp.int32)
    pairs = (amount - 1) // 2
    donor, sink = sizes[1:1 + 2 * pairs:2], sizes[2:2 + 2 * pairs:2]
    slack = jnp.minimum(donor - 1, bound - sink)
    passed = jax.random.randint(jax.random.fold_in(key, 1), (pairs,), 0, 1 << 20) % (slack + 1)
    sizes = sizes.at[1:1 + 2 * pairs:2].set(donor - passed).at[2:2 + 2 * pairs:2].set(sink + passed)
    return sizes[jax.random.permutation(jax.random.fold_in(key, 2), amount)]


def centred(rng, shape, spread, most, split=(), held_as=jnp.bfloat16):
    level = block_levels(rng, shape, split, -0.22, 0.18) if split else 1.0
    entries = jax.random.normal(rng, shape, jnp.float32) * spread * level
    return jnp.minimum(jnp.maximum(entries, -most), most).astype(held_as)


def setup_inputs(seed: int = 0) -> dict:
    streams_of = jax.random.split(jax.random.key(seed), 6)
    teacher_hidden = centred(streams_of[0], (TOKENS, DT), 1.0, 6.0, ((0, 2), (1, 2)))
    teacher_head = centred(streams_of[1], (DT, VOCAB), 0.0331, 0.19921875, ((0, 2), (1, 8)))
    student_hidden = centred(streams_of[2], (TOKENS, DS), 1.0, 6.0, ((0, 2), (1, 2)))
    student_head = centred(streams_of[3], (DS, VOCAB), 0.0541, 0.328125, ((0, 2), (1, 8)))
    live_counts = uneven_parts(streams_of[4], N_TOK, 3 * TOK_DEV * N_TOK // 4, TOK_DEV, 2).astype(jnp.int32)
    return dict(teacher_hidden=teacher_hidden, teacher_head=teacher_head, student_hidden=student_hidden, student_head=student_head, live_counts=live_counts)


def reference(teacher_hidden, teacher_head, student_hidden, student_head, live_counts):
    live_rows = (jnp.arange(TOK_DEV, dtype=jnp.int32)[None, :] < live_counts[:, None]).reshape(TOKENS).astype(jnp.float32)
    live_total = jnp.sum(live_counts.astype(jnp.float32))
    teacher = jnp.dot(teacher_hidden, teacher_head, preferred_element_type=jnp.float32) * 0.5
    student = jnp.dot(student_hidden, student_head, preferred_element_type=jnp.float32) * 0.5
    teacher_exp = jnp.exp(teacher)
    student_exp = jnp.exp(student)
    teacher_sum = jnp.sum(teacher_exp, axis=1)
    student_sum = jnp.sum(student_exp, axis=1)
    cross = jnp.sum(teacher_exp * (teacher - student), axis=1)
    divergence = cross / teacher_sum - jnp.log(teacher_sum) + jnp.log(student_sum)
    loss = jnp.sum(live_rows * divergence) / live_total
    row_scale = live_rows * (32.0 * VOCAB * 0.5 / live_total)
    logit_grad = (row_scale[:, None] * (student_exp / student_sum[:, None] - teacher_exp / teacher_sum[:, None])).astype(jnp.bfloat16)
    head_grad = jnp.dot(student_hidden.T, logit_grad, preferred_element_type=jnp.float32).astype(jnp.bfloat16)
    hidden_grad = jnp.dot(logit_grad, student_head.T, preferred_element_type=jnp.float32).astype(jnp.bfloat16)
    return (loss, head_grad, hidden_grad)
```

```python
import functools

import jax
import jax.numpy as jnp
from jax import lax
from jax.experimental import pallas as pl
from jax.experimental.pallas import tpu as pltpu
from jax.sharding import PartitionSpec as P


def softened(teacher_logits, student_logits):
    teacher = teacher_logits * 0.5
    student = student_logits * 0.5
    teacher_exp = jnp.exp(teacher)
    student_exp = jnp.exp(student)
    partial_sums = (
        jnp.sum(teacher_exp, axis=1),
        jnp.sum(student_exp, axis=1),
        jnp.sum(teacher_exp * (teacher - student), axis=1),
    )
    return (teacher_exp, student_exp, partial_sums)


def finish(teacher_exp, student_exp, totals, live_rows, live_total, vocab_entries):
    teacher_sum, student_sum, cross = totals
    divergence = cross / teacher_sum - jnp.log(teacher_sum) + jnp.log(student_sum)
    numerator = jnp.sum(live_rows * divergence)
    row_scale = live_rows * (32.0 * vocab_entries * 0.5 / live_total)
    logit_grad = (
        row_scale[:, None]
        * (student_exp / student_sum[:, None] - teacher_exp / teacher_sum[:, None])
    ).astype(jnp.bfloat16)
    return (logit_grad, numerator)


def body(teacher_hidden, teacher_head, student_hidden, student_head, live_counts):
    token_rows = teacher_hidden.shape[0]
    vocab_entries = student_head.shape[1] * lax.axis_size("vocab")
    live_total = lax.psum(jnp.sum(live_counts.astype(jnp.float32)), "tok")
    live_rows = (jnp.arange(token_rows, dtype=jnp.int32) < live_counts[0]).astype(jnp.float32)
    teacher_part = jnp.dot(teacher_hidden, teacher_head, preferred_element_type=jnp.float32)
    student_part = jnp.dot(student_hidden, student_head, preferred_element_type=jnp.float32)
    teacher_logits, student_logits = lax.psum((teacher_part, student_part), "sect")
    teacher_exp, student_exp, partial_sums = softened(teacher_logits, student_logits)
    totals = lax.psum((partial_sums[0], partial_sums[1], partial_sums[2]), "vocab")
    logit_grad, numerator = finish(
        teacher_exp, student_exp, totals, live_rows, live_total, vocab_entries
    )
    owned_features = lax.all_to_all(student_hidden, "tok", split_axis=1, concat_axis=0, tiled=True)
    head_sum = lax.dot_general(
        owned_features,
        lax.all_gather(logit_grad, "tok", axis=0, tiled=True),
        (((0,), (0,)), ((), ())),
        preferred_element_type=jnp.float32,
    )
    head_grad = head_sum.astype(jnp.bfloat16)
    hidden_grad = lax.psum_scatter(
        lax.dot_general(
            logit_grad, student_head, (((1,), (1,)), ((), ())), preferred_element_type=jnp.float32
        ),
        "vocab",
        scatter_dimension=0,
        tiled=True,
    ).astype(jnp.bfloat16)
    loss = lax.psum(numerator, "tok") / live_total
    return (loss, head_grad, hidden_grad)


MESH = pl.DeviceIdType.MESH
TILE = 32
F32, BF16 = jnp.float32, jnp.bfloat16


def fused(
    n_tok, n_voc, cw, fw,
    counts, th_hbm, thead_hbm, sh_hbm, shead_hbm,
    loss_ref, head_ref, hid_ref,
    th, thead, sh, shead, part, precv, te_ref, se_ref, stat, ssend, srecv,
    cnt, crecv, num, nrecv, hown, hrecv, grad, grecv, hs, hrv,
    load_sem, p_ss, p_rs, c_ss, c_rs, h_ss, h_rs, s_ss, s_rs, g_ss, g_rs, n_ss, n_rs, d_ss, d_rs,
):
    sect, tok, voc = lax.axis_index("sect"), lax.axis_index("tok"), lax.axis_index("vocab")
    rows, feats, width = sh.shape[0], sh.shape[1], shead.shape[1]
    block, out_rows = feats // n_tok, rows // n_voc
    chunks, f_chunks, tiles = width // cw, feats // fw, rows // TILE
    other = {"sect": 1 - sect}
    tok_peers = [(tok + d) % n_tok for d in range(1, n_tok)]
    voc_peers = [(voc + d) % n_voc for d in range(1, n_voc)]

    barrier = pltpu.get_barrier_semaphore()
    pl.semaphore_signal(barrier, inc=1, device_id=other, device_id_type=MESH)
    for p in tok_peers:
        pl.semaphore_signal(barrier, inc=1, device_id={"tok": p}, device_id_type=MESH)
    for p in voc_peers:
        pl.semaphore_signal(barrier, inc=1, device_id={"vocab": p}, device_id_type=MESH)

    loads = [
        pltpu.make_async_copy(sh_hbm, sh, load_sem.at[0]),
        pltpu.make_async_copy(shead_hbm, shead, load_sem.at[1]),
        pltpu.make_async_copy(th_hbm, th, load_sem.at[2]),
    ] + [
        pltpu.make_async_copy(
            thead_hbm.at[:, pl.ds(c * cw, cw)], thead.at[c], load_sem.at[3 + c]
        )
        for c in range(chunks)
    ]
    for load in loads:
        load.start()

    def send(src, dst, ss, rs, to):
        copy = pltpu.make_async_remote_copy(
            src_ref=src, dst_ref=dst, send_sem=ss, recv_sem=rs, device_id=to, device_id_type=MESH
        )
        copy.start()
        return copy

    cnt[...] = jnp.full(cnt.shape, counts[0].astype(F32))
    loads[0].wait()
    loads[1].wait()
    pl.semaphore_wait(barrier, n_tok + n_voc - 1)
    c_cp, h_cp, p_cp = [], [], []
    for i, p in enumerate(tok_peers):
        c_cp.append(send(cnt, crecv.at[i], c_ss.at[i], c_rs.at[i], {"tok": p}))
        cols = pl.ds(pl.multiple_of(p * block, block), block)
        h_cp.append(send(sh.at[:, cols], hrecv.at[i], h_ss.at[i], h_rs.at[i], {"tok": p}))
    for c in range(chunks):
        part[c] = jnp.dot(sh[...], shead[:, c * cw:(c + 1) * cw], preferred_element_type=F32)
        p_cp.append(send(part.at[c], precv.at[c], p_ss.at[c], p_rs.at[c], other))
    loads[2].wait()
    for c in range(chunks):
        loads[3 + c].wait()
        q = chunks + c
        part[q] = jnp.dot(th[...], thead[c], preferred_element_type=F32)
        p_cp.append(send(part.at[q], precv.at[q], p_ss.at[q], p_rs.at[q], other))
    hown[...] = sh[:, pl.ds(pl.multiple_of(tok * block, block), block)].T
    for copy in p_cp:
        copy.wait_recv()

    lane = lax.broadcasted_iota(jnp.int32, (TILE, 128), 1)

    def soften(i, carry):
        at = pl.ds(pl.multiple_of(i * TILE, TILE), TILE)
        zt = zs = cross = jnp.zeros((TILE, 1), F32)
        for c in range(chunks):
            s = (part[c, at, :] + precv[c, at, :]) * 0.5
            t = (part[chunks + c, at, :] + precv[chunks + c, at, :]) * 0.5
            te, se = jnp.exp(t), jnp.exp(s)
            te_ref[c, at, :] = te
            se_ref[c, at, :] = se
            zt += jnp.sum(te, axis=1, keepdims=True)
            zs += jnp.sum(se, axis=1, keepdims=True)
            cross += jnp.sum(te * (t - s), axis=1, keepdims=True)
        stat[at, :] = jnp.where(lane == 0, zt, jnp.where(lane == 1, zs, cross))
        return carry

    lax.fori_loop(0, tiles, soften, 0)
    ssend[...] = stat[...].T[:8]
    s_cp = [
        send(ssend, srecv.at[i], s_ss.at[i], s_rs.at[i], {"vocab": p})
        for i, p in enumerate(voc_peers)
    ]
    for copy in c_cp:
        copy.wait_recv()
    total = cnt[...]
    for i in range(n_tok - 1):
        total = total + crecv[i]
    live_total = total[0:1, 0:1]
    scale = 32.0 * (width * n_voc) * 0.5 / live_total
    mine = cnt[0:1, 0:1]
    totals = ssend[...]
    for i, copy in enumerate(s_cp):
        copy.wait_recv()
        totals = totals + srecv[i]
    stat[...] = jnp.concatenate([totals] * 16, axis=0).T

    def finish_tile(i, acc):
        at = pl.ds(pl.multiple_of(i * TILE, TILE), TILE)
        sums = stat[at, :]
        zt, zs, cross = sums[:, 0:1], sums[:, 1:2], sums[:, 2:3]
        row = (lax.broadcasted_iota(jnp.int32, (TILE, 1), 0) + i * TILE).astype(F32)
        live = (row < mine).astype(F32)
        kl = cross / zt - jnp.log(zt) + jnp.log(zs)
        a, b = live * scale / zs, live * scale / zt
        for c in range(chunks):
            g = a * se_ref[c, at, :] - b * te_ref[c, at, :]
            grad[at, c * cw:(c + 1) * cw] = g.astype(BF16)
        return acc + live * kl

    acc = lax.fori_loop(0, tiles, finish_tile, jnp.zeros((TILE, 1), F32))
    num[...] = jnp.broadcast_to(jnp.sum(acc, axis=0, keepdims=True), num.shape)
    g_cp, n_cp, d_cp = [], [], []
    for i, p in enumerate(tok_peers):
        n_cp.append(send(num, nrecv.at[i], n_ss.at[i], n_rs.at[i], {"tok": p}))
        g_cp.append(send(grad, grecv.at[i], g_ss.at[i], g_rs.at[i], {"tok": p}))
    for f in range(f_chunks):
        hs[f] = lax.dot_general(
            grad[...], shead[f * fw:(f + 1) * fw, :], (((1,), (1,)), ((), ())),
            preferred_element_type=F32,
        ).astype(BF16)
        for i, p in enumerate(voc_peers):
            at = pl.ds(pl.multiple_of(p * out_rows, out_rows), out_rows)
            d_cp.append(
                (f, i, send(hs.at[f, at, :], hrv.at[i, f], d_ss.at[i, f], d_rs.at[i, f], {"vocab": p}))
            )

    head = jnp.dot(hown[...], grad[...], preferred_element_type=F32)
    numerator = num[...]
    for i in range(n_tok - 1):
        h_cp[i].wait_recv()
        n_cp[i].wait_recv()
        numerator = numerator + nrecv[i]
        theirs = hrecv[i].T
        g_cp[i].wait_recv()
        head = head + jnp.dot(theirs, grecv[i], preferred_element_type=F32)
    head_ref[...] = head.astype(BF16)
    loss_ref[...] = numerator / live_total

    here = pl.ds(pl.multiple_of(voc * out_rows, out_rows), out_rows)
    for f in range(f_chunks):
        hid = hs[f, here, :].astype(F32)
        for g, i, copy in d_cp:
            if g == f:
                copy.wait_recv()
                hid = hid + hrv[i, f].astype(F32)
        hid_ref[:, f * fw:(f + 1) * fw] = hid.astype(BF16)
    for copy in p_cp + c_cp + h_cp + s_cp + g_cp + n_cp:
        copy.wait_send()
    for _, _, copy in d_cp:
        copy.wait_send()


def fused_body(n_tok, n_voc, teacher_hidden, teacher_head, student_hidden, student_head, live_counts):
    rows, t_feats = teacher_hidden.shape
    feats, width = student_head.shape
    cw, fw = width // 2, feats // 3
    block, out_rows = feats // n_tok, rows // n_voc
    tp, vp, nf = n_tok - 1, n_voc - 1, feats // fw
    vmem, dma = pltpu.VMEM, pltpu.SemaphoreType.DMA
    any_spec = pl.BlockSpec(memory_space=pl.ANY)
    vm_spec = pl.BlockSpec(memory_space=pltpu.VMEM)
    loss, head, hid = pl.pallas_call(
        functools.partial(fused, n_tok, n_voc, cw, fw),
        out_shape=(
            jax.ShapeDtypeStruct((8, 128), F32),
            jax.ShapeDtypeStruct((block, width), BF16),
            jax.ShapeDtypeStruct((out_rows, feats), BF16),
        ),
        in_specs=[pl.BlockSpec(memory_space=pltpu.SMEM)] + [any_spec] * 4,
        out_specs=(vm_spec,) * 3,
        scratch_shapes=[
            vmem((rows, t_feats), BF16), vmem((2, t_feats, cw), BF16),
            vmem((rows, feats), BF16), vmem((feats, width), BF16),
            vmem((4, rows, cw), F32), vmem((4, rows, cw), F32),
            vmem((2, rows, cw), F32), vmem((2, rows, cw), F32),
            vmem((rows, 128), F32), vmem((8, rows), F32), vmem((vp, 8, rows), F32),
            vmem((8, 128), F32), vmem((tp, 8, 128), F32),
            vmem((8, 128), F32), vmem((tp, 8, 128), F32),
            vmem((block, rows), BF16), vmem((tp, rows, block), BF16),
            vmem((rows, width), BF16), vmem((tp, rows, width), BF16),
            vmem((nf, rows, fw), BF16), vmem((vp, nf, out_rows, fw), BF16),
            dma((5,)), dma((4,)), dma((4,)), dma((tp,)), dma((tp,)), dma((tp,)), dma((tp,)),
            dma((vp,)), dma((vp,)), dma((tp,)), dma((tp,)), dma((tp,)), dma((tp,)),
            dma((vp, nf)), dma((vp, nf)),
        ],
        compiler_params=pltpu.CompilerParams(
            collective_id=0, has_side_effects=True, vmem_limit_bytes=48 * 1024 * 1024
        ),
    )(live_counts, teacher_hidden, teacher_head, student_hidden, student_head)
    return (loss[0, 0], head, hid)


def solution(mesh):
    placed = (P("tok", "sect"), P("sect", "vocab"), P("tok", "sect"), P("sect", "vocab"), P("tok"))
    n_tok, n_voc = mesh.shape["tok"], mesh.shape["vocab"]

    def run(*args):
        rows = args[0].shape[0]
        if rows % (TILE * n_voc) == 0 and n_tok > 1:
            return fused_body(n_tok, n_voc, *args)
        return body(*args)

    return jax.shard_map(
        run,
        mesh=mesh,
        in_specs=placed,
        out_specs=(P(), P(("sect", "tok"), "vocab"), P(("tok", "vocab"), "sect")),
        check_vma=False,
    )
```

```python
import functools

import jax
import jax.numpy as jnp
from jax import lax
from jax.experimental import pallas as pl
from jax.experimental.pallas import tpu as pltpu
from jax.sharding import PartitionSpec as P


def softened(teacher_logits, student_logits):
    teacher = teacher_logits * 0.5
    student = student_logits * 0.5
    teacher_exp = jnp.exp(teacher)
    student_exp = jnp.exp(student)
    partial_sums = (
        jnp.sum(teacher_exp, axis=1),
        jnp.sum(student_exp, axis=1),
        jnp.sum(teacher_exp * (teacher - student), axis=1),
    )
    return (teacher_exp, student_exp, partial_sums)


def finish(teacher_exp, student_exp, totals, live_rows, live_total, vocab_entries):
    teacher_sum, student_sum, cross = totals
    divergence = cross / teacher_sum - jnp.log(teacher_sum) + jnp.log(student_sum)
    numerator = jnp.sum(live_rows * divergence)
    row_scale = live_rows * (32.0 * vocab_entries * 0.5 / live_total)
    logit_grad = (
        row_scale[:, None]
        * (student_exp / student_sum[:, None] - teacher_exp / teacher_sum[:, None])
    ).astype(jnp.bfloat16)
    return (logit_grad, numerator)


def body(teacher_hidden, teacher_head, student_hidden, student_head, live_counts):
    token_rows = teacher_hidden.shape[0]
    vocab_entries = student_head.shape[1] * lax.axis_size("vocab")
    live_total = lax.psum(jnp.sum(live_counts.astype(jnp.float32)), "tok")
    live_rows = (jnp.arange(token_rows, dtype=jnp.int32) < live_counts[0]).astype(jnp.float32)
    teacher_part = jnp.dot(teacher_hidden, teacher_head, preferred_element_type=jnp.float32)
    student_part = jnp.dot(student_hidden, student_head, preferred_element_type=jnp.float32)
    teacher_logits, student_logits = lax.psum((teacher_part, student_part), "sect")
    teacher_exp, student_exp, partial_sums = softened(teacher_logits, student_logits)
    totals = lax.psum((partial_sums[0], partial_sums[1], partial_sums[2]), "vocab")
    logit_grad, numerator = finish(
        teacher_exp, student_exp, totals, live_rows, live_total, vocab_entries
    )
    owned_features = lax.all_to_all(student_hidden, "tok", split_axis=1, concat_axis=0, tiled=True)
    head_sum = lax.dot_general(
        owned_features,
        lax.all_gather(logit_grad, "tok", axis=0, tiled=True),
        (((0,), (0,)), ((), ())),
        preferred_element_type=jnp.float32,
    )
    head_grad = head_sum.astype(jnp.bfloat16)
    hidden_grad = lax.psum_scatter(
        lax.dot_general(
            logit_grad, student_head, (((1,), (1,)), ((), ())), preferred_element_type=jnp.float32
        ),
        "vocab",
        scatter_dimension=0,
        tiled=True,
    ).astype(jnp.bfloat16)
    loss = lax.psum(numerator, "tok") / live_total
    return (loss, head_grad, hidden_grad)


MESH = pl.DeviceIdType.MESH
TILE = 32
F32, BF16 = jnp.float32, jnp.bfloat16


def fused(
    n_tok, n_in, n_out, cw, fw,
    counts, th_hbm, thead_hbm, sh_hbm, shead_hbm,
    loss_ref, head_ref, hid_ref,
    th, thead, sh, shead, part, precv, te_ref, se_ref, stat, ssend, srecv,
    cnt, crecv, num, nrecv, hown, hrecv, grad, grecv, head_acc, hf, hs, yr, hp, zb, zr,
    load_sem, p_ss, p_rs, c_ss, c_rs, h_ss, h_rs, s_ss, s_rs, g_ss, g_rs, n_ss, n_rs,
    y_ss, y_rs, z_ss, z_rs,
):
    sect, tok, voc = lax.axis_index("sect"), lax.axis_index("tok"), lax.axis_index("vocab")
    rows, feats, width = sh.shape[0], sh.shape[1], shead.shape[1]
    n_voc = n_in * n_out
    inner, outer = voc % n_in, voc // n_in
    in_peers = [(inner + d) % n_in for d in range(1, n_in)]
    out_peers = [(outer + d) % n_out for d in range(1, n_out)]
    block, out_rows = feats // n_tok, rows // n_voc
    chunks, f_chunks, tiles = width // cw, feats // fw, rows // TILE
    other = {"sect": 1 - sect}
    tok_peers = [(tok + d) % n_tok for d in range(1, n_tok)]
    voc_peers = [(voc + d) % n_voc for d in range(1, n_voc)]

    barrier = pltpu.get_barrier_semaphore()
    pl.semaphore_signal(barrier, inc=1, device_id=other, device_id_type=MESH)
    for p in tok_peers:
        pl.semaphore_signal(barrier, inc=1, device_id={"tok": p}, device_id_type=MESH)
    for p in voc_peers:
        pl.semaphore_signal(barrier, inc=1, device_id={"vocab": p}, device_id_type=MESH)

    loads = [
        pltpu.make_async_copy(sh_hbm, sh, load_sem.at[0]),
        pltpu.make_async_copy(shead_hbm, shead, load_sem.at[1]),
        pltpu.make_async_copy(th_hbm, th, load_sem.at[2]),
    ] + [
        pltpu.make_async_copy(
            thead_hbm.at[:, pl.ds(c * cw, cw)], thead.at[c], load_sem.at[3 + c]
        )
        for c in range(chunks)
    ]
    for load in loads:
        load.start()

    def send(src, dst, ss, rs, to):
        copy = pltpu.make_async_remote_copy(
            src_ref=src, dst_ref=dst, send_sem=ss, recv_sem=rs, device_id=to, device_id_type=MESH
        )
        copy.start()
        return copy

    cnt[...] = jnp.full(cnt.shape, counts[0].astype(F32))
    loads[0].wait()
    loads[1].wait()
    pl.semaphore_wait(barrier, n_tok + n_voc - 1)
    c_cp, h_cp, p_cp = [], [], []
    for i, p in enumerate(tok_peers):
        c_cp.append(send(cnt, crecv.at[i], c_ss.at[i], c_rs.at[i], {"tok": p}))
        cols = pl.ds(pl.multiple_of(p * block, block), block)
        h_cp.append(send(sh.at[:, cols], hrecv.at[i], h_ss.at[i], h_rs.at[i], {"tok": p}))
    for c in range(chunks):
        part[c] = jnp.dot(sh[...], shead[:, c * cw:(c + 1) * cw], preferred_element_type=F32)
        p_cp.append(send(part.at[c], precv.at[c], p_ss.at[c], p_rs.at[c], other))
    loads[2].wait()
    for c in range(chunks):
        loads[3 + c].wait()
        q = chunks + c
        part[q] = jnp.dot(th[...], thead[c], preferred_element_type=F32)
        p_cp.append(send(part.at[q], precv.at[q], p_ss.at[q], p_rs.at[q], other))
    hown[...] = sh[:, pl.ds(pl.multiple_of(tok * block, block), block)].T
    for copy in p_cp:
        copy.wait_recv()

    lane = lax.broadcasted_iota(jnp.int32, (TILE, 128), 1)

    def soften(i, carry):
        at = pl.ds(pl.multiple_of(i * TILE, TILE), TILE)
        zt = zs = cross = jnp.zeros((TILE, 1), F32)
        for c in range(chunks):
            s = (part[c, at, :] + precv[c, at, :]) * 0.5
            t = (part[chunks + c, at, :] + precv[chunks + c, at, :]) * 0.5
            te, se = jnp.exp(t), jnp.exp(s)
            te_ref[c, at, :] = te
            se_ref[c, at, :] = se
            zt += jnp.sum(te, axis=1, keepdims=True)
            zs += jnp.sum(se, axis=1, keepdims=True)
            cross += jnp.sum(te * (t - s), axis=1, keepdims=True)
        stat[at, :] = jnp.where(lane == 0, zt, jnp.where(lane == 1, zs, cross))
        return carry

    lax.fori_loop(0, tiles, soften, 0)
    ssend[...] = stat[...].T[:8]
    s_cp = [
        send(ssend, srecv.at[i], s_ss.at[i], s_rs.at[i], {"vocab": p})
        for i, p in enumerate(voc_peers)
    ]
    for copy in c_cp:
        copy.wait_recv()
    total = cnt[...]
    for i in range(n_tok - 1):
        total = total + crecv[i]
    live_total = total[0:1, 0:1]
    scale = 32.0 * (width * n_voc) * 0.5 / live_total
    mine = cnt[0:1, 0:1]
    totals = ssend[...]
    for i, copy in enumerate(s_cp):
        copy.wait_recv()
        totals = totals + srecv[i]
    stat[...] = jnp.concatenate([totals] * 16, axis=0).T

    def finish_tile(i, acc):
        at = pl.ds(pl.multiple_of(i * TILE, TILE), TILE)
        sums = stat[at, :]
        zt, zs, cross = sums[:, 0:1], sums[:, 1:2], sums[:, 2:3]
        row = (lax.broadcasted_iota(jnp.int32, (TILE, 1), 0) + i * TILE).astype(F32)
        live = (row < mine).astype(F32)
        kl = cross / zt - jnp.log(zt) + jnp.log(zs)
        a, b = live * scale / zs, live * scale / zt
        for c in range(chunks):
            g = a * se_ref[c, at, :] - b * te_ref[c, at, :]
            grad[at, c * cw:(c + 1) * cw] = g.astype(BF16)
        return acc + live * kl

    acc = lax.fori_loop(0, tiles, finish_tile, jnp.zeros((TILE, 1), F32))
    num[...] = jnp.broadcast_to(jnp.sum(acc, axis=0, keepdims=True), num.shape)
    g_cp, n_cp, y_cp, z_cp = [], [], [], []
    for f in range(f_chunks):
        term = lax.dot_general(
            grad[...], shead[f * fw:(f + 1) * fw, :], (((1,), (1,)), ((), ())),
            preferred_element_type=F32,
        ).reshape(n_out, n_in, out_rows, fw)
        hf[f] = term
        hs[f] = term.astype(BF16)
        for i, p in enumerate(in_peers):
            y_cp.append(
                send(hs.at[f, :, p], yr.at[i, f], y_ss.at[i, f], y_rs.at[i, f],
                     {"vocab": outer * n_in + p})
            )
        if f == 0:
            for i, p in enumerate(tok_peers):
                n_cp.append(send(num, nrecv.at[i], n_ss.at[i], n_rs.at[i], {"tok": p}))
                g_cp.append(send(grad, grecv.at[i], g_ss.at[i], g_rs.at[i], {"tok": p}))

    head_acc[...] = jnp.dot(hown[...], grad[...], preferred_element_type=F32)
    for f in range(f_chunks):
        pair = hf[f, :, inner]
        for i in range(n_in - 1):
            y_cp[f * (n_in - 1) + i].wait_recv()
            pair = pair + yr[i, f].astype(F32)
        hp[f] = pair
        zb[f] = pair.astype(BF16)
        for i, p in enumerate(out_peers):
            z_cp.append(
                send(zb.at[f, p], zr.at[i, f], z_ss.at[i, f], z_rs.at[i, f],
                     {"vocab": p * n_in + inner})
            )

    head = head_acc[...]
    numerator = num[...]
    for i in range(n_tok - 1):
        h_cp[i].wait_recv()
        n_cp[i].wait_recv()
        numerator = numerator + nrecv[i]
        theirs = hrecv[i].T
        g_cp[i].wait_recv()
        head = head + jnp.dot(theirs, grecv[i], preferred_element_type=F32)
    head_ref[...] = head.astype(BF16)
    loss_ref[...] = numerator / live_total

    for f in range(f_chunks):
        hid = hp[f, outer]
        for i in range(n_out - 1):
            z_cp[f * (n_out - 1) + i].wait_recv()
            hid = hid + zr[i, f].astype(F32)
        hid_ref[:, f * fw:(f + 1) * fw] = hid.astype(BF16)
    for copy in p_cp + c_cp + h_cp + s_cp + g_cp + n_cp + y_cp + z_cp:
        copy.wait_send()


def fused_body(n_tok, n_voc, teacher_hidden, teacher_head, student_hidden, student_head, live_counts):
    rows, t_feats = teacher_hidden.shape
    feats, width = student_head.shape
    cw, fw = width // 2, feats // 3
    block, out_rows = feats // n_tok, rows // n_voc
    n_in, n_out = 2, n_voc // 2
    tp, vp, ip, op, nf = n_tok - 1, n_voc - 1, n_in - 1, n_out - 1, feats // fw
    vmem, dma = pltpu.VMEM, pltpu.SemaphoreType.DMA
    any_spec = pl.BlockSpec(memory_space=pl.ANY)
    vm_spec = pl.BlockSpec(memory_space=pltpu.VMEM)
    loss, head, hid = pl.pallas_call(
        functools.partial(fused, n_tok, n_in, n_out, cw, fw),
        out_shape=(
            jax.ShapeDtypeStruct((8, 128), F32),
            jax.ShapeDtypeStruct((block, width), BF16),
            jax.ShapeDtypeStruct((out_rows, feats), BF16),
        ),
        in_specs=[pl.BlockSpec(memory_space=pltpu.SMEM)] + [any_spec] * 4,
        out_specs=(vm_spec,) * 3,
        scratch_shapes=[
            vmem((rows, t_feats), BF16), vmem((2, t_feats, cw), BF16),
            vmem((rows, feats), BF16), vmem((feats, width), BF16),
            vmem((4, rows, cw), F32), vmem((4, rows, cw), F32),
            vmem((2, rows, cw), F32), vmem((2, rows, cw), F32),
            vmem((rows, 128), F32), vmem((8, rows), F32), vmem((vp, 8, rows), F32),
            vmem((8, 128), F32), vmem((tp, 8, 128), F32),
            vmem((8, 128), F32), vmem((tp, 8, 128), F32),
            vmem((block, rows), BF16), vmem((tp, rows, block), BF16),
            vmem((rows, width), BF16), vmem((tp, rows, width), BF16),
            vmem((block, width), F32),
            vmem((nf, n_out, n_in, out_rows, fw), F32), vmem((nf, n_out, n_in, out_rows, fw), BF16),
            vmem((ip, nf, n_out, out_rows, fw), BF16),
            vmem((nf, n_out, out_rows, fw), F32), vmem((nf, n_out, out_rows, fw), BF16),
            vmem((op, nf, out_rows, fw), BF16),
            dma((5,)), dma((4,)), dma((4,)), dma((tp,)), dma((tp,)), dma((tp,)), dma((tp,)),
            dma((vp,)), dma((vp,)), dma((tp,)), dma((tp,)), dma((tp,)), dma((tp,)),
            dma((ip, nf)), dma((ip, nf)), dma((op, nf)), dma((op, nf)),
        ],
        compiler_params=pltpu.CompilerParams(
            collective_id=0, has_side_effects=True, vmem_limit_bytes=60 * 1024 * 1024
        ),
    )(live_counts, teacher_hidden, teacher_head, student_hidden, student_head)
    return (loss[0, 0], head, hid)


def solution(mesh):
    placed = (P("tok", "sect"), P("sect", "vocab"), P("tok", "sect"), P("sect", "vocab"), P("tok"))
    n_tok, n_voc = mesh.shape["tok"], mesh.shape["vocab"]

    def run(*args):
        rows = args[0].shape[0]
        if rows % (TILE * n_voc) == 0 and n_voc % 2 == 0 and n_voc > 2 and n_tok > 1:
            return fused_body(n_tok, n_voc, *args)
        return body(*args)

    return jax.shard_map(
        run,
        mesh=mesh,
        in_specs=placed,
        out_specs=(P(), P(("sect", "tok"), "vocab"), P(("tok", "vocab"), "sect")),
        check_vma=False,
    )
```

```python
import functools

import jax
import jax.numpy as jnp
from jax import lax
from jax.experimental import pallas as pl
from jax.experimental.pallas import tpu as pltpu
from jax.sharding import PartitionSpec as P


def softened(teacher_logits, student_logits):
    teacher = teacher_logits * 0.5
    student = student_logits * 0.5
    teacher_exp = jnp.exp(teacher)
    student_exp = jnp.exp(student)
    partial_sums = (
        jnp.sum(teacher_exp, axis=1),
        jnp.sum(student_exp, axis=1),
        jnp.sum(teacher_exp * (teacher - student), axis=1),
    )
    return (teacher_exp, student_exp, partial_sums)


def finish(teacher_exp, student_exp, totals, live_rows, live_total, vocab_entries):
    teacher_sum, student_sum, cross = totals
    divergence = cross / teacher_sum - jnp.log(teacher_sum) + jnp.log(student_sum)
    numerator = jnp.sum(live_rows * divergence)
    row_scale = live_rows * (32.0 * vocab_entries * 0.5 / live_total)
    logit_grad = (
        row_scale[:, None]
        * (student_exp / student_sum[:, None] - teacher_exp / teacher_sum[:, None])
    ).astype(jnp.bfloat16)
    return (logit_grad, numerator)


def body(teacher_hidden, teacher_head, student_hidden, student_head, live_counts):
    token_rows = teacher_hidden.shape[0]
    vocab_entries = student_head.shape[1] * lax.axis_size("vocab")
    live_total = lax.psum(jnp.sum(live_counts.astype(jnp.float32)), "tok")
    live_rows = (jnp.arange(token_rows, dtype=jnp.int32) < live_counts[0]).astype(jnp.float32)
    teacher_part = jnp.dot(teacher_hidden, teacher_head, preferred_element_type=jnp.float32)
    student_part = jnp.dot(student_hidden, student_head, preferred_element_type=jnp.float32)
    teacher_logits, student_logits = lax.psum((teacher_part, student_part), "sect")
    teacher_exp, student_exp, partial_sums = softened(teacher_logits, student_logits)
    totals = lax.psum((partial_sums[0], partial_sums[1], partial_sums[2]), "vocab")
    logit_grad, numerator = finish(
        teacher_exp, student_exp, totals, live_rows, live_total, vocab_entries
    )
    owned_features = lax.all_to_all(student_hidden, "tok", split_axis=1, concat_axis=0, tiled=True)
    head_sum = lax.dot_general(
        owned_features,
        lax.all_gather(logit_grad, "tok", axis=0, tiled=True),
        (((0,), (0,)), ((), ())),
        preferred_element_type=jnp.float32,
    )
    head_grad = head_sum.astype(jnp.bfloat16)
    hidden_grad = lax.psum_scatter(
        lax.dot_general(
            logit_grad, student_head, (((1,), (1,)), ((), ())), preferred_element_type=jnp.float32
        ),
        "vocab",
        scatter_dimension=0,
        tiled=True,
    ).astype(jnp.bfloat16)
    loss = lax.psum(numerator, "tok") / live_total
    return (loss, head_grad, hidden_grad)


MESH = pl.DeviceIdType.MESH
TILE = 32
F32, BF16 = jnp.float32, jnp.bfloat16


def fused(
    n_tok, n_in, n_out, cw, fw,
    counts, th_hbm, thead_hbm, sh_hbm, shead_hbm,
    loss_ref, head_ref, hid_ref,
    th, thead, sh, shead, part, precv, te_ref, se_ref, stat, ssend, srecv,
    cnt, crecv, num, nrecv, hown, hrecv, grad, grecv, head_acc, hf, hs, yr, hp, zb, zr,
    load_sem, p_ss, p_rs, c_ss, c_rs, h_ss, h_rs, s_ss, s_rs, g_ss, g_rs, n_ss, n_rs,
    y_ss, y_rs, z_ss, z_rs,
):
    sect, tok, voc = lax.axis_index("sect"), lax.axis_index("tok"), lax.axis_index("vocab")
    rows, feats, width = sh.shape[0], sh.shape[1], shead.shape[1]
    n_voc = n_in * n_out
    inner, outer = voc % n_in, voc // n_in
    in_peers = [(inner + d) % n_in for d in range(1, n_in)]
    out_peers = [(outer + d) % n_out for d in range(1, n_out)]
    block, out_rows = feats // n_tok, rows // n_voc
    chunks, f_chunks, tiles = width // cw, feats // fw, rows // TILE
    other = {"sect": 1 - sect}
    tok_peers = [(tok + d) % n_tok for d in range(1, n_tok)]
    voc_peers = [(voc + d) % n_voc for d in range(1, n_voc)]

    barrier = pltpu.get_barrier_semaphore()
    pl.semaphore_signal(barrier, inc=1, device_id=other, device_id_type=MESH)
    for p in tok_peers:
        pl.semaphore_signal(barrier, inc=1, device_id={"tok": p}, device_id_type=MESH)
    for p in voc_peers:
        pl.semaphore_signal(barrier, inc=1, device_id={"vocab": p}, device_id_type=MESH)

    loads = [
        pltpu.make_async_copy(sh_hbm, sh, load_sem.at[0]),
        pltpu.make_async_copy(shead_hbm, shead, load_sem.at[1]),
        pltpu.make_async_copy(th_hbm, th, load_sem.at[2]),
    ] + [
        pltpu.make_async_copy(
            thead_hbm.at[:, pl.ds(c * cw, cw)], thead.at[c], load_sem.at[3 + c]
        )
        for c in range(chunks)
    ]
    for load in loads:
        load.start()

    def send(src, dst, ss, rs, to):
        copy = pltpu.make_async_remote_copy(
            src_ref=src, dst_ref=dst, send_sem=ss, recv_sem=rs, device_id=to, device_id_type=MESH
        )
        copy.start()
        return copy

    cnt[...] = jnp.full(cnt.shape, counts[0].astype(F32))
    loads[0].wait()
    loads[1].wait()
    for c in range(chunks):
        part[c] = jnp.dot(sh[...], shead[:, c * cw:(c + 1) * cw], preferred_element_type=F32)
    pl.semaphore_wait(barrier, n_tok + n_voc - 1)
    c_cp, h_cp, p_cp = [], [], []
    for c in range(chunks):
        p_cp.append(send(part.at[c], precv.at[c], p_ss.at[c], p_rs.at[c], other))
    for i, p in enumerate(tok_peers):
        c_cp.append(send(cnt, crecv.at[i], c_ss.at[i], c_rs.at[i], {"tok": p}))
        cols = pl.ds(pl.multiple_of(p * block, block), block)
        h_cp.append(send(sh.at[:, cols], hrecv.at[i], h_ss.at[i], h_rs.at[i], {"tok": p}))
    loads[2].wait()
    for c in range(chunks):
        loads[3 + c].wait()
        q = chunks + c
        part[q] = jnp.dot(th[...], thead[c], preferred_element_type=F32)
        p_cp.append(send(part.at[q], precv.at[q], p_ss.at[q], p_rs.at[q], other))
    hown[...] = sh[:, pl.ds(pl.multiple_of(tok * block, block), block)].T
    for copy in p_cp:
        copy.wait_recv()

    lane = lax.broadcasted_iota(jnp.int32, (TILE, 128), 1)

    def soften(i, carry):
        at = pl.ds(pl.multiple_of(i * TILE, TILE), TILE)
        zt = zs = cross = jnp.zeros((TILE, 1), F32)
        for c in range(chunks):
            s = (part[c, at, :] + precv[c, at, :]) * 0.5
            t = (part[chunks + c, at, :] + precv[chunks + c, at, :]) * 0.5
            te, se = jnp.exp(t), jnp.exp(s)
            te_ref[c, at, :] = te
            se_ref[c, at, :] = se
            zt += jnp.sum(te, axis=1, keepdims=True)
            zs += jnp.sum(se, axis=1, keepdims=True)
            cross += jnp.sum(te * (t - s), axis=1, keepdims=True)
        stat[at, :] = jnp.where(lane == 0, zt, jnp.where(lane == 1, zs, cross))
        return carry

    lax.fori_loop(0, tiles, soften, 0)
    ssend[...] = stat[...].T[:8]
    s_cp = [
        send(ssend, srecv.at[i], s_ss.at[i], s_rs.at[i], {"vocab": p})
        for i, p in enumerate(voc_peers)
    ]
    for copy in c_cp:
        copy.wait_recv()
    total = cnt[...]
    for i in range(n_tok - 1):
        total = total + crecv[i]
    live_total = total[0:1, 0:1]
    scale = 32.0 * (width * n_voc) * 0.5 / live_total
    mine = cnt[0:1, 0:1]
    totals = ssend[...]
    for i, copy in enumerate(s_cp):
        copy.wait_recv()
        totals = totals + srecv[i]
    stat[...] = jnp.concatenate([totals] * 16, axis=0).T

    def finish_tile(i, acc):
        at = pl.ds(pl.multiple_of(i * TILE, TILE), TILE)
        sums = stat[at, :]
        zt, zs, cross = sums[:, 0:1], sums[:, 1:2], sums[:, 2:3]
        row = (lax.broadcasted_iota(jnp.int32, (TILE, 1), 0) + i * TILE).astype(F32)
        live = (row < mine).astype(F32)
        kl = cross / zt - jnp.log(zt) + jnp.log(zs)
        a, b = live * scale / zs, live * scale / zt
        for c in range(chunks):
            g = a * se_ref[c, at, :] - b * te_ref[c, at, :]
            grad[at, c * cw:(c + 1) * cw] = g.astype(BF16)
        return acc + live * kl

    acc = lax.fori_loop(0, tiles, finish_tile, jnp.zeros((TILE, 1), F32))
    num[...] = jnp.broadcast_to(jnp.sum(acc, axis=0, keepdims=True), num.shape)
    g_cp, n_cp, y_cp, z_cp = [], [], [], []
    for f in range(f_chunks):
        term = lax.dot_general(
            grad[...], shead[f * fw:(f + 1) * fw, :], (((1,), (1,)), ((), ())),
            preferred_element_type=F32,
        ).reshape(n_out, n_in, out_rows, fw)
        hf[f] = term
        hs[f] = term.astype(BF16)
        for i, p in enumerate(in_peers):
            y_cp.append(
                send(hs.at[f, :, p], yr.at[i, f], y_ss.at[i, f], y_rs.at[i, f],
                     {"vocab": outer * n_in + p})
            )
        if f == 0:
            for i, p in enumerate(tok_peers):
                n_cp.append(send(num, nrecv.at[i], n_ss.at[i], n_rs.at[i], {"tok": p}))
                g_cp.append(send(grad, grecv.at[i], g_ss.at[i], g_rs.at[i], {"tok": p}))

    head_acc[...] = jnp.dot(hown[...], grad[...], preferred_element_type=F32)
    for f in range(f_chunks):
        pair = hf[f, :, inner]
        for i in range(n_in - 1):
            y_cp[f * (n_in - 1) + i].wait_recv()
            pair = pair + yr[i, f].astype(F32)
        hp[f] = pair
        zb[f] = pair.astype(BF16)
        for i, p in enumerate(out_peers):
            z_cp.append(
                send(zb.at[f, p], zr.at[i, f], z_ss.at[i, f], z_rs.at[i, f],
                     {"vocab": p * n_in + inner})
            )

    head = head_acc[...]
    numerator = num[...]
    for i in range(n_tok - 1):
        h_cp[i].wait_recv()
        n_cp[i].wait_recv()
        numerator = numerator + nrecv[i]
        theirs = hrecv[i].T
        g_cp[i].wait_recv()
        head = head + jnp.dot(theirs, grecv[i], preferred_element_type=F32)
    head_ref[...] = head.astype(BF16)
    loss_ref[...] = numerator / live_total

    for f in range(f_chunks):
        hid = hp[f, outer]
        for i in range(n_out - 1):
            z_cp[f * (n_out - 1) + i].wait_recv()
            hid = hid + zr[i, f].astype(F32)
        hid_ref[:, f * fw:(f + 1) * fw] = hid.astype(BF16)
    for copy in p_cp + c_cp + h_cp + s_cp + g_cp + n_cp + y_cp + z_cp:
        copy.wait_send()


def fused_body(n_tok, n_voc, teacher_hidden, teacher_head, student_hidden, student_head, live_counts):
    rows, t_feats = teacher_hidden.shape
    feats, width = student_head.shape
    cw, fw = width // 2, feats // 6
    block, out_rows = feats // n_tok, rows // n_voc
    n_in, n_out = 2, n_voc // 2
    tp, vp, ip, op, nf = n_tok - 1, n_voc - 1, n_in - 1, n_out - 1, feats // fw
    vmem, dma = pltpu.VMEM, pltpu.SemaphoreType.DMA
    any_spec = pl.BlockSpec(memory_space=pl.ANY)
    vm_spec = pl.BlockSpec(memory_space=pltpu.VMEM)
    loss, head, hid = pl.pallas_call(
        functools.partial(fused, n_tok, n_in, n_out, cw, fw),
        out_shape=(
            jax.ShapeDtypeStruct((8, 128), F32),
            jax.ShapeDtypeStruct((block, width), BF16),
            jax.ShapeDtypeStruct((out_rows, feats), BF16),
        ),
        in_specs=[pl.BlockSpec(memory_space=pltpu.SMEM)] + [any_spec] * 4,
        out_specs=(vm_spec,) * 3,
        scratch_shapes=[
            vmem((rows, t_feats), BF16), vmem((2, t_feats, cw), BF16),
            vmem((rows, feats), BF16), vmem((feats, width), BF16),
            vmem((4, rows, cw), F32), vmem((4, rows, cw), F32),
            vmem((2, rows, cw), F32), vmem((2, rows, cw), F32),
            vmem((rows, 128), F32), vmem((8, rows), F32), vmem((vp, 8, rows), F32),
            vmem((8, 128), F32), vmem((tp, 8, 128), F32),
            vmem((8, 128), F32), vmem((tp, 8, 128), F32),
            vmem((block, rows), BF16), vmem((tp, rows, block), BF16),
            vmem((rows, width), BF16), vmem((tp, rows, width), BF16),
            vmem((block, width), F32),
            vmem((nf, n_out, n_in, out_rows, fw), F32), vmem((nf, n_out, n_in, out_rows, fw), BF16),
            vmem((ip, nf, n_out, out_rows, fw), BF16),
            vmem((nf, n_out, out_rows, fw), F32), vmem((nf, n_out, out_rows, fw), BF16),
            vmem((op, nf, out_rows, fw), BF16),
            dma((5,)), dma((4,)), dma((4,)), dma((tp,)), dma((tp,)), dma((tp,)), dma((tp,)),
            dma((vp,)), dma((vp,)), dma((tp,)), dma((tp,)), dma((tp,)), dma((tp,)),
            dma((ip, nf)), dma((ip, nf)), dma((op, nf)), dma((op, nf)),
        ],
        compiler_params=pltpu.CompilerParams(
            collective_id=0, has_side_effects=True, vmem_limit_bytes=53 * 1024 * 1024
        ),
    )(live_counts, teacher_hidden, teacher_head, student_hidden, student_head)
    return (loss[0, 0], head, hid)


def solution(mesh):
    placed = (P("tok", "sect"), P("sect", "vocab"), P("tok", "sect"), P("sect", "vocab"), P("tok"))
    n_tok, n_voc = mesh.shape["tok"], mesh.shape["vocab"]

    def run(*args):
        rows = args[0].shape[0]
        if rows % (TILE * n_voc) == 0 and n_voc % 2 == 0 and n_voc > 2 and n_tok > 1:
            return fused_body(n_tok, n_voc, *args)
        return body(*args)

    return jax.shard_map(
        run,
        mesh=mesh,
        in_specs=placed,
        out_specs=(P(), P(("sect", "tok"), "vocab"), P(("tok", "vocab"), "sect")),
        check_vma=False,
    )
```

```python
import functools

import jax
import jax.numpy as jnp
from jax import lax
from jax.experimental import pallas as pl
from jax.experimental.pallas import tpu as pltpu
from jax.sharding import PartitionSpec as P


def softened(teacher_logits, student_logits):
    teacher = teacher_logits * 0.5
    student = student_logits * 0.5
    teacher_exp = jnp.exp(teacher)
    student_exp = jnp.exp(student)
    partial_sums = (
        jnp.sum(teacher_exp, axis=1),
        jnp.sum(student_exp, axis=1),
        jnp.sum(teacher_exp * (teacher - student), axis=1),
    )
    return (teacher_exp, student_exp, partial_sums)


def finish(teacher_exp, student_exp, totals, live_rows, live_total, vocab_entries):
    teacher_sum, student_sum, cross = totals
    divergence = cross / teacher_sum - jnp.log(teacher_sum) + jnp.log(student_sum)
    numerator = jnp.sum(live_rows * divergence)
    row_scale = live_rows * (32.0 * vocab_entries * 0.5 / live_total)
    logit_grad = (
        row_scale[:, None]
        * (student_exp / student_sum[:, None] - teacher_exp / teacher_sum[:, None])
    ).astype(jnp.bfloat16)
    return (logit_grad, numerator)


def body(teacher_hidden, teacher_head, student_hidden, student_head, live_counts):
    token_rows = teacher_hidden.shape[0]
    vocab_entries = student_head.shape[1] * lax.axis_size("vocab")
    live_total = lax.psum(jnp.sum(live_counts.astype(jnp.float32)), "tok")
    live_rows = (jnp.arange(token_rows, dtype=jnp.int32) < live_counts[0]).astype(jnp.float32)
    teacher_part = jnp.dot(teacher_hidden, teacher_head, preferred_element_type=jnp.float32)
    student_part = jnp.dot(student_hidden, student_head, preferred_element_type=jnp.float32)
    teacher_logits, student_logits = lax.psum((teacher_part, student_part), "sect")
    teacher_exp, student_exp, partial_sums = softened(teacher_logits, student_logits)
    totals = lax.psum((partial_sums[0], partial_sums[1], partial_sums[2]), "vocab")
    logit_grad, numerator = finish(
        teacher_exp, student_exp, totals, live_rows, live_total, vocab_entries
    )
    owned_features = lax.all_to_all(student_hidden, "tok", split_axis=1, concat_axis=0, tiled=True)
    head_sum = lax.dot_general(
        owned_features,
        lax.all_gather(logit_grad, "tok", axis=0, tiled=True),
        (((0,), (0,)), ((), ())),
        preferred_element_type=jnp.float32,
    )
    head_grad = head_sum.astype(jnp.bfloat16)
    hidden_grad = lax.psum_scatter(
        lax.dot_general(
            logit_grad, student_head, (((1,), (1,)), ((), ())), preferred_element_type=jnp.float32
        ),
        "vocab",
        scatter_dimension=0,
        tiled=True,
    ).astype(jnp.bfloat16)
    loss = lax.psum(numerator, "tok") / live_total
    return (loss, head_grad, hidden_grad)


MESH = pl.DeviceIdType.MESH
TILE = 32
F32, BF16 = jnp.float32, jnp.bfloat16


def fused(
    n_tok, n_in, n_out, cw, fw,
    counts, th_hbm, thead_hbm, sh_hbm, shead_hbm,
    loss_ref, head_ref, hid_ref,
    th, thead, sh, shead, part, precv, te_ref, se_ref, stat, ssend, srecv,
    cnt, crecv, num, nrecv, hown, hrecv, grad, grecv, head_acc, hf, hs, yr, hp, zb, zr,
    load_sem, p_ss, p_rs, c_ss, c_rs, h_ss, h_rs, s_ss, s_rs, g_ss, g_rs, n_ss, n_rs,
    y_ss, y_rs, z_ss, z_rs,
):
    sect, tok, voc = lax.axis_index("sect"), lax.axis_index("tok"), lax.axis_index("vocab")
    rows, feats, width = sh.shape[0], sh.shape[1], shead.shape[1]
    n_voc = n_in * n_out
    inner, outer = voc % n_in, voc // n_in
    in_peers = [(inner + d) % n_in for d in range(1, n_in)]
    out_peers = [(outer + d) % n_out for d in range(1, n_out)]
    block, out_rows = feats // n_tok, rows // n_voc
    chunks, f_chunks, tiles = width // cw, feats // fw, rows // TILE
    other = {"sect": 1 - sect}
    tok_peers = [(tok + d) % n_tok for d in range(1, n_tok)]
    voc_peers = [(voc + d) % n_voc for d in range(1, n_voc)]

    barrier = pltpu.get_barrier_semaphore()
    pl.semaphore_signal(barrier, inc=1, device_id=other, device_id_type=MESH)
    for p in tok_peers:
        pl.semaphore_signal(barrier, inc=1, device_id={"tok": p}, device_id_type=MESH)
    for p in voc_peers:
        pl.semaphore_signal(barrier, inc=1, device_id={"vocab": p}, device_id_type=MESH)

    loads = [
        pltpu.make_async_copy(sh_hbm, sh, load_sem.at[0]),
        pltpu.make_async_copy(shead_hbm, shead, load_sem.at[1]),
        pltpu.make_async_copy(th_hbm, th, load_sem.at[2]),
    ] + [
        pltpu.make_async_copy(
            thead_hbm.at[:, pl.ds(c * cw, cw)], thead.at[c], load_sem.at[3 + c]
        )
        for c in range(chunks)
    ]
    for load in loads:
        load.start()

    def send(src, dst, ss, rs, to):
        copy = pltpu.make_async_remote_copy(
            src_ref=src, dst_ref=dst, send_sem=ss, recv_sem=rs, device_id=to, device_id_type=MESH
        )
        copy.start()
        return copy

    cnt[...] = jnp.full(cnt.shape, counts[0].astype(F32))
    loads[0].wait()
    loads[1].wait()
    for c in range(chunks):
        part[c] = jnp.dot(sh[...], shead[:, c * cw:(c + 1) * cw], preferred_element_type=F32)
    pl.semaphore_wait(barrier, n_tok + n_voc - 1)
    c_cp, h_cp, p_cp = [], [], []
    for c in range(chunks):
        p_cp.append(send(part.at[c], precv.at[c], p_ss.at[c], p_rs.at[c], other))
    for i, p in enumerate(tok_peers):
        c_cp.append(send(cnt, crecv.at[i], c_ss.at[i], c_rs.at[i], {"tok": p}))
        cols = pl.ds(pl.multiple_of(p * block, block), block)
        h_cp.append(send(sh.at[:, cols], hrecv.at[i], h_ss.at[i], h_rs.at[i], {"tok": p}))
    loads[2].wait()
    for c in range(chunks):
        loads[3 + c].wait()
        q = chunks + c
        part[q] = jnp.dot(th[...], thead[c], preferred_element_type=F32)
        p_cp.append(send(part.at[q], precv.at[q], p_ss.at[q], p_rs.at[q], other))
    for copy in p_cp:
        copy.wait_recv()

    lane = lax.broadcasted_iota(jnp.int32, (TILE, 128), 1)

    def soften(i, carry):
        at = pl.ds(pl.multiple_of(i * TILE, TILE), TILE)
        zt = zs = cross = jnp.zeros((TILE, 1), F32)
        for c in range(chunks):
            s = (part[c, at, :] + precv[c, at, :]) * 0.5
            t = (part[chunks + c, at, :] + precv[chunks + c, at, :]) * 0.5
            te, se = jnp.exp(t), jnp.exp(s)
            te_ref[c, at, :] = te
            se_ref[c, at, :] = se
            zt += jnp.sum(te, axis=1, keepdims=True)
            zs += jnp.sum(se, axis=1, keepdims=True)
            cross += jnp.sum(te * (t - s), axis=1, keepdims=True)
        stat[at, :] = jnp.where(lane == 0, zt, jnp.where(lane == 1, zs, cross))
        return carry

    lax.fori_loop(0, tiles, soften, 0)
    ssend[...] = stat[...].T[:8]
    s_cp = [
        send(ssend, srecv.at[i], s_ss.at[i], s_rs.at[i], {"vocab": p})
        for i, p in enumerate(voc_peers)
    ]
    hown[...] = sh[:, pl.ds(pl.multiple_of(tok * block, block), block)].T
    for copy in c_cp:
        copy.wait_recv()
    total = cnt[...]
    for i in range(n_tok - 1):
        total = total + crecv[i]
    live_total = total[0:1, 0:1]
    scale = 32.0 * (width * n_voc) * 0.5 / live_total
    mine = cnt[0:1, 0:1]
    totals = ssend[...]
    for i, copy in enumerate(s_cp):
        copy.wait_recv()
        totals = totals + srecv[i]
    stat[...] = jnp.concatenate([totals] * 16, axis=0).T

    def finish_tile(i, acc):
        at = pl.ds(pl.multiple_of(i * TILE, TILE), TILE)
        sums = stat[at, :]
        zt, zs, cross = sums[:, 0:1], sums[:, 1:2], sums[:, 2:3]
        row = (lax.broadcasted_iota(jnp.int32, (TILE, 1), 0) + i * TILE).astype(F32)
        live = (row < mine).astype(F32)
        kl = cross / zt - jnp.log(zt) + jnp.log(zs)
        a, b = live * scale / zs, live * scale / zt
        for c in range(chunks):
            g = a * se_ref[c, at, :] - b * te_ref[c, at, :]
            grad[at, c * cw:(c + 1) * cw] = g.astype(BF16)
        return acc + live * kl

    acc = lax.fori_loop(0, tiles, finish_tile, jnp.zeros((TILE, 1), F32))
    num[...] = jnp.broadcast_to(jnp.sum(acc, axis=0, keepdims=True), num.shape)
    g_cp, n_cp, y_cp, z_cp = [], [], [], []
    for f in range(f_chunks):
        term = lax.dot_general(
            grad[...], shead[f * fw:(f + 1) * fw, :], (((1,), (1,)), ((), ())),
            preferred_element_type=F32,
        ).reshape(n_out, n_in, out_rows, fw)
        hf[f] = term
        hs[f] = term.astype(BF16)
        for i, p in enumerate(in_peers):
            y_cp.append(
                send(hs.at[f, :, p], yr.at[i, f], y_ss.at[i, f], y_rs.at[i, f],
                     {"vocab": outer * n_in + p})
            )
        if f == 0:
            for i, p in enumerate(tok_peers):
                n_cp.append(send(num, nrecv.at[i], n_ss.at[i], n_rs.at[i], {"tok": p}))
                g_cp.append(send(grad, grecv.at[i], g_ss.at[i], g_rs.at[i], {"tok": p}))

    for f in range(f_chunks):
        pair = hf[f, :, inner]
        for i in range(n_in - 1):
            y_cp[f * (n_in - 1) + i].wait_recv()
            pair = pair + yr[i, f].astype(F32)
        hp[f] = pair
        zb[f] = pair.astype(BF16)
        for i, p in enumerate(out_peers):
            z_cp.append(
                send(zb.at[f, p], zr.at[i, f], z_ss.at[i, f], z_rs.at[i, f],
                     {"vocab": p * n_in + inner})
            )
        if f == f_chunks // 2:
            head_acc[...] = jnp.dot(hown[...], grad[...], preferred_element_type=F32)

    head = head_acc[...]
    numerator = num[...]
    for i in range(n_tok - 1):
        h_cp[i].wait_recv()
        n_cp[i].wait_recv()
        numerator = numerator + nrecv[i]
        theirs = hrecv[i].T
        g_cp[i].wait_recv()
        head = head + jnp.dot(theirs, grecv[i], preferred_element_type=F32)
    head_ref[...] = head.astype(BF16)
    loss_ref[...] = numerator / live_total

    for f in range(f_chunks):
        hid = hp[f, outer]
        for i in range(n_out - 1):
            z_cp[f * (n_out - 1) + i].wait_recv()
            hid = hid + zr[i, f].astype(F32)
        hid_ref[:, f * fw:(f + 1) * fw] = hid.astype(BF16)
    for copy in p_cp + c_cp + h_cp + s_cp + g_cp + n_cp + y_cp + z_cp:
        copy.wait_send()


def fused_body(n_tok, n_voc, teacher_hidden, teacher_head, student_hidden, student_head, live_counts):
    rows, t_feats = teacher_hidden.shape
    feats, width = student_head.shape
    cw, fw = width // 2, feats // 6
    block, out_rows = feats // n_tok, rows // n_voc
    n_in, n_out = 2, n_voc // 2
    tp, vp, ip, op, nf = n_tok - 1, n_voc - 1, n_in - 1, n_out - 1, feats // fw
    vmem, dma = pltpu.VMEM, pltpu.SemaphoreType.DMA
    any_spec = pl.BlockSpec(memory_space=pl.ANY)
    vm_spec = pl.BlockSpec(memory_space=pltpu.VMEM)
    loss, head, hid = pl.pallas_call(
        functools.partial(fused, n_tok, n_in, n_out, cw, fw),
        out_shape=(
            jax.ShapeDtypeStruct((8, 128), F32),
            jax.ShapeDtypeStruct((block, width), BF16),
            jax.ShapeDtypeStruct((out_rows, feats), BF16),
        ),
        in_specs=[pl.BlockSpec(memory_space=pltpu.SMEM)] + [any_spec] * 4,
        out_specs=(vm_spec,) * 3,
        scratch_shapes=[
            vmem((rows, t_feats), BF16), vmem((2, t_feats, cw), BF16),
            vmem((rows, feats), BF16), vmem((feats, width), BF16),
            vmem((4, rows, cw), F32), vmem((4, rows, cw), F32),
            vmem((2, rows, cw), F32), vmem((2, rows, cw), F32),
            vmem((rows, 128), F32), vmem((8, rows), F32), vmem((vp, 8, rows), F32),
            vmem((8, 128), F32), vmem((tp, 8, 128), F32),
            vmem((8, 128), F32), vmem((tp, 8, 128), F32),
            vmem((block, rows), BF16), vmem((tp, rows, block), BF16),
            vmem((rows, width), BF16), vmem((tp, rows, width), BF16),
            vmem((block, width), F32),
            vmem((nf, n_out, n_in, out_rows, fw), F32), vmem((nf, n_out, n_in, out_rows, fw), BF16),
            vmem((ip, nf, n_out, out_rows, fw), BF16),
            vmem((nf, n_out, out_rows, fw), F32), vmem((nf, n_out, out_rows, fw), BF16),
            vmem((op, nf, out_rows, fw), BF16),
            dma((5,)), dma((4,)), dma((4,)), dma((tp,)), dma((tp,)), dma((tp,)), dma((tp,)),
            dma((vp,)), dma((vp,)), dma((tp,)), dma((tp,)), dma((tp,)), dma((tp,)),
            dma((ip, nf)), dma((ip, nf)), dma((op, nf)), dma((op, nf)),
        ],
        compiler_params=pltpu.CompilerParams(
            collective_id=0, has_side_effects=True, vmem_limit_bytes=53 * 1024 * 1024
        ),
    )(live_counts, teacher_hidden, teacher_head, student_hidden, student_head)
    return (loss[0, 0], head, hid)


def solution(mesh):
    placed = (P("tok", "sect"), P("sect", "vocab"), P("tok", "sect"), P("sect", "vocab"), P("tok"))
    n_tok, n_voc = mesh.shape["tok"], mesh.shape["vocab"]

    def run(*args):
        rows = args[0].shape[0]
        if rows % (TILE * n_voc) == 0 and n_voc % 2 == 0 and n_voc > 2 and n_tok > 1:
            return fused_body(n_tok, n_voc, *args)
        return body(*args)

    return jax.shard_map(
        run,
        mesh=mesh,
        in_specs=placed,
        out_specs=(P(), P(("sect", "tok"), "vocab"), P(("tok", "vocab"), "sect")),
        check_vma=False,
    )
```

```python
import functools

import jax
import jax.numpy as jnp
from jax import lax
from jax.experimental import pallas as pl
from jax.experimental.pallas import tpu as pltpu
from jax.sharding import PartitionSpec as P


def softened(teacher_logits, student_logits):
    teacher = teacher_logits * 0.5
    student = student_logits * 0.5
    teacher_exp = jnp.exp(teacher)
    student_exp = jnp.exp(student)
    partial_sums = (
        jnp.sum(teacher_exp, axis=1),
        jnp.sum(student_exp, axis=1),
        jnp.sum(teacher_exp * (teacher - student), axis=1),
    )
    return (teacher_exp, student_exp, partial_sums)


def finish(teacher_exp, student_exp, totals, live_rows, live_total, vocab_entries):
    teacher_sum, student_sum, cross = totals
    divergence = cross / teacher_sum - jnp.log(teacher_sum) + jnp.log(student_sum)
    numerator = jnp.sum(live_rows * divergence)
    row_scale = live_rows * (32.0 * vocab_entries * 0.5 / live_total)
    logit_grad = (
        row_scale[:, None]
        * (student_exp / student_sum[:, None] - teacher_exp / teacher_sum[:, None])
    ).astype(jnp.bfloat16)
    return (logit_grad, numerator)


def body(teacher_hidden, teacher_head, student_hidden, student_head, live_counts):
    token_rows = teacher_hidden.shape[0]
    vocab_entries = student_head.shape[1] * lax.axis_size("vocab")
    live_total = lax.psum(jnp.sum(live_counts.astype(jnp.float32)), "tok")
    live_rows = (jnp.arange(token_rows, dtype=jnp.int32) < live_counts[0]).astype(jnp.float32)
    teacher_part = jnp.dot(teacher_hidden, teacher_head, preferred_element_type=jnp.float32)
    student_part = jnp.dot(student_hidden, student_head, preferred_element_type=jnp.float32)
    teacher_logits, student_logits = lax.psum((teacher_part, student_part), "sect")
    teacher_exp, student_exp, partial_sums = softened(teacher_logits, student_logits)
    totals = lax.psum((partial_sums[0], partial_sums[1], partial_sums[2]), "vocab")
    logit_grad, numerator = finish(
        teacher_exp, student_exp, totals, live_rows, live_total, vocab_entries
    )
    owned_features = lax.all_to_all(student_hidden, "tok", split_axis=1, concat_axis=0, tiled=True)
    head_sum = lax.dot_general(
        owned_features,
        lax.all_gather(logit_grad, "tok", axis=0, tiled=True),
        (((0,), (0,)), ((), ())),
        preferred_element_type=jnp.float32,
    )
    head_grad = head_sum.astype(jnp.bfloat16)
    hidden_grad = lax.psum_scatter(
        lax.dot_general(
            logit_grad, student_head, (((1,), (1,)), ((), ())), preferred_element_type=jnp.float32
        ),
        "vocab",
        scatter_dimension=0,
        tiled=True,
    ).astype(jnp.bfloat16)
    loss = lax.psum(numerator, "tok") / live_total
    return (loss, head_grad, hidden_grad)


MESH = pl.DeviceIdType.MESH
TILE = 32
F32, BF16 = jnp.float32, jnp.bfloat16


def fused(
    n_tok, n_in, n_out, cw, fw,
    counts, th_hbm, thead_hbm, sh_hbm, shead_hbm,
    loss_ref, head_ref, hid_ref,
    th, thead, sh, shead, part, precv, te_ref, se_ref, stat, ssend, srecv,
    cnt, crecv, num, nrecv, hown, hrecv, grad, grecv, head_acc, hf, hs, yr, hp, zb, zr,
    load_sem, p_ss, p_rs, c_ss, c_rs, h_ss, h_rs, s_ss, s_rs, g_ss, g_rs, n_ss, n_rs,
    y_ss, y_rs, z_ss, z_rs,
):
    sect, tok, voc = lax.axis_index("sect"), lax.axis_index("tok"), lax.axis_index("vocab")
    rows, feats, width = sh.shape[0], sh.shape[1], shead.shape[1]
    n_voc = n_in * n_out
    inner, outer = voc % n_in, voc // n_in
    in_peers = [(inner + d) % n_in for d in range(1, n_in)]
    out_peers = [(outer + d) % n_out for d in range(1, n_out)]
    block, out_rows = feats // n_tok, rows // n_voc
    chunks, f_chunks, tiles = width // cw, feats // fw, rows // TILE
    other = {"sect": 1 - sect}
    tok_peers = [(tok + d) % n_tok for d in range(1, n_tok)]
    voc_peers = [(voc + d) % n_voc for d in range(1, n_voc)]

    barrier = pltpu.get_barrier_semaphore()
    pl.semaphore_signal(barrier, inc=1, device_id=other, device_id_type=MESH)
    for p in tok_peers:
        pl.semaphore_signal(barrier, inc=1, device_id={"tok": p}, device_id_type=MESH)
    for p in voc_peers:
        pl.semaphore_signal(barrier, inc=1, device_id={"vocab": p}, device_id_type=MESH)

    loads = [
        pltpu.make_async_copy(sh_hbm, sh, load_sem.at[0]),
        pltpu.make_async_copy(shead_hbm, shead, load_sem.at[1]),
        pltpu.make_async_copy(th_hbm, th, load_sem.at[2]),
    ] + [
        pltpu.make_async_copy(
            thead_hbm.at[:, pl.ds(c * cw, cw)], thead.at[c], load_sem.at[3 + c]
        )
        for c in range(chunks)
    ]
    for load in loads:
        load.start()

    def send(src, dst, ss, rs, to):
        copy = pltpu.make_async_remote_copy(
            src_ref=src, dst_ref=dst, send_sem=ss, recv_sem=rs, device_id=to, device_id_type=MESH
        )
        copy.start()
        return copy

    cnt[...] = jnp.full(cnt.shape, counts[0].astype(F32))
    loads[0].wait()
    loads[1].wait()
    for c in range(chunks):
        part[c] = jnp.dot(sh[...], shead[:, c * cw:(c + 1) * cw], preferred_element_type=F32)
    pl.semaphore_wait(barrier, n_tok + n_voc - 1)
    c_cp, h_cp, p_cp = [], [], []
    for c in range(chunks):
        p_cp.append(send(part.at[c], precv.at[c], p_ss.at[c], p_rs.at[c], other))
    for i, p in enumerate(tok_peers):
        c_cp.append(send(cnt, crecv.at[i], c_ss.at[i], c_rs.at[i], {"tok": p}))
        cols = pl.ds(pl.multiple_of(p * block, block), block)
        h_cp.append(send(sh.at[:, cols], hrecv.at[i], h_ss.at[i], h_rs.at[i], {"tok": p}))
    loads[2].wait()
    for c in range(chunks):
        loads[3 + c].wait()
        q = chunks + c
        part[q] = jnp.dot(th[...], thead[c], preferred_element_type=F32)
        p_cp.append(send(part.at[q], precv.at[q], p_ss.at[q], p_rs.at[q], other))
    for copy in p_cp:
        copy.wait_recv()

    lane = lax.broadcasted_iota(jnp.int32, (TILE, 128), 1)

    def soften(i, carry):
        at = pl.ds(pl.multiple_of(i * TILE, TILE), TILE)
        zt = zs = cross = jnp.zeros((TILE, 1), F32)
        for c in range(chunks):
            s = (part[c, at, :] + precv[c, at, :]) * 0.5
            t = (part[chunks + c, at, :] + precv[chunks + c, at, :]) * 0.5
            te, se = jnp.exp(t), jnp.exp(s)
            te_ref[c, at, :] = te
            se_ref[c, at, :] = se
            zt += jnp.sum(te, axis=1, keepdims=True)
            zs += jnp.sum(se, axis=1, keepdims=True)
            cross += jnp.sum(te * (t - s), axis=1, keepdims=True)
        stat[at, :] = jnp.where(lane == 0, zt, jnp.where(lane == 1, zs, cross))
        return carry

    lax.fori_loop(0, tiles, soften, 0)
    ssend[...] = stat[...].T[:8]
    s_cp = [
        send(ssend, srecv.at[i], s_ss.at[i], s_rs.at[i], {"vocab": p})
        for i, p in enumerate(voc_peers)
    ]
    hown[...] = sh[:, pl.ds(pl.multiple_of(tok * block, block), block)].T
    for copy in c_cp:
        copy.wait_recv()
    total = cnt[...]
    for i in range(n_tok - 1):
        total = total + crecv[i]
    live_total = total[0:1, 0:1]
    scale = 32.0 * (width * n_voc) * 0.5 / live_total
    mine = cnt[0:1, 0:1]
    totals = ssend[...]
    for i, copy in enumerate(s_cp):
        copy.wait_recv()
        totals = totals + srecv[i]
    stat[...] = jnp.concatenate([totals] * 16, axis=0).T

    def finish_tile(i, acc):
        at = pl.ds(pl.multiple_of(i * TILE, TILE), TILE)
        sums = stat[at, :]
        zt, zs, cross = sums[:, 0:1], sums[:, 1:2], sums[:, 2:3]
        row = (lax.broadcasted_iota(jnp.int32, (TILE, 1), 0) + i * TILE).astype(F32)
        live = (row < mine).astype(F32)
        kl = cross / zt - jnp.log(zt) + jnp.log(zs)
        a, b = live * scale / zs, live * scale / zt
        for c in range(chunks):
            g = a * se_ref[c, at, :] - b * te_ref[c, at, :]
            grad[at, c * cw:(c + 1) * cw] = g.astype(BF16)
        return acc + live * kl

    acc = lax.fori_loop(0, tiles, finish_tile, jnp.zeros((TILE, 1), F32))
    num[...] = jnp.broadcast_to(jnp.sum(acc, axis=0, keepdims=True), num.shape)
    g_cp, n_cp, y_cp, z_cp = [], [], [], []
    for f in range(f_chunks):
        term = lax.dot_general(
            grad[...], shead[f * fw:(f + 1) * fw, :], (((1,), (1,)), ((), ())),
            preferred_element_type=F32,
        ).reshape(n_out, n_in, out_rows, fw)
        hf[f] = term
        hs[f] = term.astype(BF16)
        for i, p in enumerate(in_peers):
            y_cp.append(
                send(hs.at[f, :, p], yr.at[i, f], y_ss.at[i, f], y_rs.at[i, f],
                     {"vocab": outer * n_in + p})
            )
        if f == 0:
            for i, p in enumerate(tok_peers):
                n_cp.append(send(num, nrecv.at[i], n_ss.at[i], n_rs.at[i], {"tok": p}))
                g_cp.append(send(grad, grecv.at[i], g_ss.at[i], g_rs.at[i], {"tok": p}))

    for f in range(f_chunks):
        pair = hf[f, :, inner]
        for i in range(n_in - 1):
            y_cp[f * (n_in - 1) + i].wait_recv()
            pair = pair + yr[i, f].astype(F32)
        hp[f] = pair
        zb[f] = pair.astype(BF16)
        for i, p in enumerate(out_peers):
            z_cp.append(
                send(zb.at[f, p], zr.at[i, f], z_ss.at[i, f], z_rs.at[i, f],
                     {"vocab": p * n_in + inner})
            )
        if f == f_chunks // 2:
            head_acc[...] = jnp.dot(hown[...], grad[...], preferred_element_type=F32)

    head = head_acc[...]
    numerator = num[...]
    for i in range(n_tok - 1):
        h_cp[i].wait_recv()
        n_cp[i].wait_recv()
        numerator = numerator + nrecv[i]
        theirs = hrecv[i].T
        g_cp[i].wait_recv()
        head = head + jnp.dot(theirs, grecv[i], preferred_element_type=F32)
    head_ref[...] = head.astype(BF16)
    loss_ref[...] = numerator / live_total

    for f in range(f_chunks):
        hid = hp[f, outer]
        for i in range(n_out - 1):
            z_cp[f * (n_out - 1) + i].wait_recv()
            hid = hid + zr[i, f].astype(F32)
        hid_ref[:, f * fw:(f + 1) * fw] = hid.astype(BF16)
    for copy in p_cp + c_cp + h_cp + s_cp + g_cp + n_cp + y_cp + z_cp:
        copy.wait_send()


def emit(loss_in, head_in, hid_in, loss_out, head_out, hid_out, sems):
    copies = [
        pltpu.make_async_copy(head_in, head_out, sems.at[0]),
        pltpu.make_async_copy(hid_in, hid_out, sems.at[1]),
    ]
    for copy in copies:
        copy.start()
    loss_out[...] = loss_in[0:1, 0:1]
    for copy in copies:
        copy.wait()


def fused_body(n_tok, n_voc, teacher_hidden, teacher_head, student_hidden, student_head, live_counts):
    rows, t_feats = teacher_hidden.shape
    feats, width = student_head.shape
    cw, fw = width // 2, feats // 6
    block, out_rows = feats // n_tok, rows // n_voc
    n_in, n_out = 2, n_voc // 2
    tp, vp, ip, op, nf = n_tok - 1, n_voc - 1, n_in - 1, n_out - 1, feats // fw
    vmem, dma = pltpu.VMEM, pltpu.SemaphoreType.DMA
    any_spec = pl.BlockSpec(memory_space=pl.ANY)
    vm_spec = pl.BlockSpec(memory_space=pltpu.VMEM)
    loss, head, hid = pl.pallas_call(
        functools.partial(fused, n_tok, n_in, n_out, cw, fw),
        out_shape=(
            jax.ShapeDtypeStruct((8, 128), F32),
            jax.ShapeDtypeStruct((block, width), BF16),
            jax.ShapeDtypeStruct((out_rows, feats), BF16),
        ),
        in_specs=[pl.BlockSpec(memory_space=pltpu.SMEM)] + [any_spec] * 4,
        out_specs=(vm_spec,) * 3,
        scratch_shapes=[
            vmem((rows, t_feats), BF16), vmem((2, t_feats, cw), BF16),
            vmem((rows, feats), BF16), vmem((feats, width), BF16),
            vmem((4, rows, cw), F32), vmem((4, rows, cw), F32),
            vmem((2, rows, cw), F32), vmem((2, rows, cw), F32),
            vmem((rows, 128), F32), vmem((8, rows), F32), vmem((vp, 8, rows), F32),
            vmem((8, 128), F32), vmem((tp, 8, 128), F32),
            vmem((8, 128), F32), vmem((tp, 8, 128), F32),
            vmem((block, rows), BF16), vmem((tp, rows, block), BF16),
            vmem((rows, width), BF16), vmem((tp, rows, width), BF16),
            vmem((block, width), F32),
            vmem((nf, n_out, n_in, out_rows, fw), F32), vmem((nf, n_out, n_in, out_rows, fw), BF16),
            vmem((ip, nf, n_out, out_rows, fw), BF16),
            vmem((nf, n_out, out_rows, fw), F32), vmem((nf, n_out, out_rows, fw), BF16),
            vmem((op, nf, out_rows, fw), BF16),
            dma((5,)), dma((4,)), dma((4,)), dma((tp,)), dma((tp,)), dma((tp,)), dma((tp,)),
            dma((vp,)), dma((vp,)), dma((tp,)), dma((tp,)), dma((tp,)), dma((tp,)),
            dma((ip, nf)), dma((ip, nf)), dma((op, nf)), dma((op, nf)),
        ],
        compiler_params=pltpu.CompilerParams(
            collective_id=0, has_side_effects=True, vmem_limit_bytes=53 * 1024 * 1024
        ),
    )(live_counts, teacher_hidden, teacher_head, student_hidden, student_head)
    loss, head, hid = pl.pallas_call(
        emit,
        out_shape=(
            jax.ShapeDtypeStruct((1, 1), F32),
            jax.ShapeDtypeStruct(head.shape, BF16),
            jax.ShapeDtypeStruct(hid.shape, BF16),
        ),
        in_specs=[vm_spec, any_spec, any_spec],
        out_specs=(vm_spec, any_spec, any_spec),
        scratch_shapes=[dma((2,))],
        compiler_params=pltpu.CompilerParams(vmem_limit_bytes=4 * 1024 * 1024),
    )(loss, head, hid)
    return (loss[0, 0], head, hid)


def solution(mesh):
    placed = (P("tok", "sect"), P("sect", "vocab"), P("tok", "sect"), P("sect", "vocab"), P("tok"))
    n_tok, n_voc = mesh.shape["tok"], mesh.shape["vocab"]

    def run(*args):
        rows = args[0].shape[0]
        if rows % (TILE * n_voc) == 0 and n_voc % 2 == 0 and n_voc > 2 and n_tok > 1:
            return fused_body(n_tok, n_voc, *args)
        return body(*args)

    return jax.shard_map(
        run,
        mesh=mesh,
        in_specs=placed,
        out_specs=(P(), P(("sect", "tok"), "vocab"), P(("tok", "vocab"), "sect")),
        check_vma=False,
    )
```

```python
import functools

import jax
import jax.numpy as jnp
from jax import lax
from jax.experimental import pallas as pl
from jax.experimental.pallas import tpu as pltpu
from jax.sharding import PartitionSpec as P


def softened(teacher_logits, student_logits):
    teacher = teacher_logits * 0.5
    student = student_logits * 0.5
    teacher_exp = jnp.exp(teacher)
    student_exp = jnp.exp(student)
    partial_sums = (
        jnp.sum(teacher_exp, axis=1),
        jnp.sum(student_exp, axis=1),
        jnp.sum(teacher_exp * (teacher - student), axis=1),
    )
    return (teacher_exp, student_exp, partial_sums)


def finish(teacher_exp, student_exp, totals, live_rows, live_total, vocab_entries):
    teacher_sum, student_sum, cross = totals
    divergence = cross / teacher_sum - jnp.log(teacher_sum) + jnp.log(student_sum)
    numerator = jnp.sum(live_rows * divergence)
    row_scale = live_rows * (32.0 * vocab_entries * 0.5 / live_total)
    logit_grad = (
        row_scale[:, None]
        * (student_exp / student_sum[:, None] - teacher_exp / teacher_sum[:, None])
    ).astype(jnp.bfloat16)
    return (logit_grad, numerator)


def body(teacher_hidden, teacher_head, student_hidden, student_head, live_counts):
    token_rows = teacher_hidden.shape[0]
    vocab_entries = student_head.shape[1] * lax.axis_size("vocab")
    live_total = lax.psum(jnp.sum(live_counts.astype(jnp.float32)), "tok")
    live_rows = (jnp.arange(token_rows, dtype=jnp.int32) < live_counts[0]).astype(jnp.float32)
    teacher_part = jnp.dot(teacher_hidden, teacher_head, preferred_element_type=jnp.float32)
    student_part = jnp.dot(student_hidden, student_head, preferred_element_type=jnp.float32)
    teacher_logits, student_logits = lax.psum((teacher_part, student_part), "sect")
    teacher_exp, student_exp, partial_sums = softened(teacher_logits, student_logits)
    totals = lax.psum((partial_sums[0], partial_sums[1], partial_sums[2]), "vocab")
    logit_grad, numerator = finish(
        teacher_exp, student_exp, totals, live_rows, live_total, vocab_entries
    )
    owned_features = lax.all_to_all(student_hidden, "tok", split_axis=1, concat_axis=0, tiled=True)
    head_sum = lax.dot_general(
        owned_features,
        lax.all_gather(logit_grad, "tok", axis=0, tiled=True),
        (((0,), (0,)), ((), ())),
        preferred_element_type=jnp.float32,
    )
    head_grad = head_sum.astype(jnp.bfloat16)
    hidden_grad = lax.psum_scatter(
        lax.dot_general(
            logit_grad, student_head, (((1,), (1,)), ((), ())), preferred_element_type=jnp.float32
        ),
        "vocab",
        scatter_dimension=0,
        tiled=True,
    ).astype(jnp.bfloat16)
    loss = lax.psum(numerator, "tok") / live_total
    return (loss, head_grad, hidden_grad)


MESH = pl.DeviceIdType.MESH
TILE = 32
F32, BF16 = jnp.float32, jnp.bfloat16


def fused(
    n_tok, n_in, n_out, cw, fw,
    counts, th_hbm, thead_hbm, sh_hbm, shead_hbm,
    loss_ref, head_ref, hid_ref,
    th, thead, sh, shead, part, precv, te_ref, se_ref, stat, ssend, srecv,
    cnt, crecv, num, nrecv, hown, hrecv, grad, grecv, head_acc, hf, hs, yr, hp, zb, zr,
    load_sem, p_ss, p_rs, c_ss, c_rs, h_ss, h_rs, s_ss, s_rs, g_ss, g_rs, n_ss, n_rs,
    y_ss, y_rs, z_ss, z_rs,
):
    sect, tok, voc = lax.axis_index("sect"), lax.axis_index("tok"), lax.axis_index("vocab")
    rows, feats, width = sh.shape[0], sh.shape[1], shead.shape[1]
    n_voc = n_in * n_out
    inner, outer = voc % n_in, voc // n_in
    in_peers = [(inner + d) % n_in for d in range(1, n_in)]
    out_peers = [(outer + d) % n_out for d in range(1, n_out)]
    block, out_rows = feats // n_tok, rows // n_voc
    chunks, f_chunks, tiles = width // cw, feats // fw, rows // TILE
    other = {"sect": 1 - sect}
    tok_peers = [(tok + d) % n_tok for d in range(1, n_tok)]
    voc_peers = [(voc + d) % n_voc for d in range(1, n_voc)]

    barrier = pltpu.get_barrier_semaphore()
    pl.semaphore_signal(barrier, inc=1, device_id=other, device_id_type=MESH)
    for p in tok_peers:
        pl.semaphore_signal(barrier, inc=1, device_id={"tok": p}, device_id_type=MESH)
    for p in voc_peers:
        pl.semaphore_signal(barrier, inc=1, device_id={"vocab": p}, device_id_type=MESH)

    loads = [
        pltpu.make_async_copy(sh_hbm, sh, load_sem.at[0]),
        pltpu.make_async_copy(shead_hbm, shead, load_sem.at[1]),
        pltpu.make_async_copy(th_hbm, th, load_sem.at[2]),
    ] + [
        pltpu.make_async_copy(
            thead_hbm.at[:, pl.ds(c * cw, cw)], thead.at[c], load_sem.at[3 + c]
        )
        for c in range(chunks)
    ]
    for load in loads:
        load.start()

    def send(src, dst, ss, rs, to):
        copy = pltpu.make_async_remote_copy(
            src_ref=src, dst_ref=dst, send_sem=ss, recv_sem=rs, device_id=to, device_id_type=MESH
        )
        copy.start()
        return copy

    cnt[...] = jnp.full(cnt.shape, counts[0].astype(F32))
    loads[0].wait()
    loads[1].wait()
    for c in range(chunks):
        part[c] = jnp.dot(sh[...], shead[:, c * cw:(c + 1) * cw], preferred_element_type=F32)
    pl.semaphore_wait(barrier, n_tok + n_voc - 1)
    c_cp, h_cp, p_cp = [], [], []
    for c in range(chunks):
        p_cp.append(send(part.at[c], precv.at[c], p_ss.at[c], p_rs.at[c], other))
    for i, p in enumerate(tok_peers):
        c_cp.append(send(cnt, crecv.at[i], c_ss.at[i], c_rs.at[i], {"tok": p}))
        cols = pl.ds(pl.multiple_of(p * block, block), block)
        h_cp.append(send(sh.at[:, cols], hrecv.at[i], h_ss.at[i], h_rs.at[i], {"tok": p}))
    loads[2].wait()
    for c in range(chunks):
        loads[3 + c].wait()
        q = chunks + c
        part[q] = jnp.dot(th[...], thead[c], preferred_element_type=F32)
        p_cp.append(send(part.at[q], precv.at[q], p_ss.at[q], p_rs.at[q], other))
    for copy in p_cp:
        copy.wait_recv()

    lane = lax.broadcasted_iota(jnp.int32, (TILE, 128), 1)

    def soften(i, carry):
        at = pl.ds(pl.multiple_of(i * TILE, TILE), TILE)
        zt = zs = cross = jnp.zeros((TILE, 1), F32)
        for c in range(chunks):
            s = (part[c, at, :] + precv[c, at, :]) * 0.5
            t = (part[chunks + c, at, :] + precv[chunks + c, at, :]) * 0.5
            te, se = jnp.exp(t), jnp.exp(s)
            te_ref[c, at, :] = te
            se_ref[c, at, :] = se
            zt += jnp.sum(te, axis=1, keepdims=True)
            zs += jnp.sum(se, axis=1, keepdims=True)
            cross += jnp.sum(te * (t - s), axis=1, keepdims=True)
        stat[at, :] = jnp.where(lane == 0, zt, jnp.where(lane == 1, zs, cross))
        return carry

    lax.fori_loop(0, tiles, soften, 0)
    ssend[...] = stat[...].T[:8]
    s_cp = [
        send(ssend, srecv.at[i], s_ss.at[i], s_rs.at[i], {"vocab": p})
        for i, p in enumerate(voc_peers)
    ]
    hown[...] = sh[:, pl.ds(pl.multiple_of(tok * block, block), block)].T
    for copy in c_cp:
        copy.wait_recv()
    total = cnt[...]
    for i in range(n_tok - 1):
        total = total + crecv[i]
    live_total = total[0:1, 0:1]
    scale = 32.0 * (width * n_voc) * 0.5 / live_total
    mine = cnt[0:1, 0:1]
    totals = ssend[...]
    for i, copy in enumerate(s_cp):
        copy.wait_recv()
        totals = totals + srecv[i]
    stat[...] = jnp.concatenate([totals] * 16, axis=0).T

    def finish_tile(i, acc):
        at = pl.ds(pl.multiple_of(i * TILE, TILE), TILE)
        sums = stat[at, :]
        zt, zs, cross = sums[:, 0:1], sums[:, 1:2], sums[:, 2:3]
        row = (lax.broadcasted_iota(jnp.int32, (TILE, 1), 0) + i * TILE).astype(F32)
        live = (row < mine).astype(F32)
        kl = cross / zt - jnp.log(zt) + jnp.log(zs)
        a, b = live * scale / zs, live * scale / zt
        for c in range(chunks):
            g = a * se_ref[c, at, :] - b * te_ref[c, at, :]
            grad[at, c * cw:(c + 1) * cw] = g.astype(BF16)
        return acc + live * kl

    acc = lax.fori_loop(0, tiles, finish_tile, jnp.zeros((TILE, 1), F32))
    num[...] = jnp.broadcast_to(jnp.sum(acc, axis=0, keepdims=True), num.shape)
    g_cp, n_cp, y_cp, z_cp = [], [], [], []
    for f in range(f_chunks):
        term = lax.dot_general(
            grad[...], shead[f * fw:(f + 1) * fw, :], (((1,), (1,)), ((), ())),
            preferred_element_type=F32,
        ).reshape(n_out, n_in, out_rows, fw)
        hf[f] = term
        hs[f] = term.astype(BF16)
        for i, p in enumerate(in_peers):
            y_cp.append(
                send(hs.at[f, :, p], yr.at[i, f], y_ss.at[i, f], y_rs.at[i, f],
                     {"vocab": outer * n_in + p})
            )
        if f == 0:
            for i, p in enumerate(tok_peers):
                n_cp.append(send(num, nrecv.at[i], n_ss.at[i], n_rs.at[i], {"tok": p}))
                g_cp.append(send(grad, grecv.at[i], g_ss.at[i], g_rs.at[i], {"tok": p}))

    for f in range(f_chunks):
        pair = hf[f, :, inner]
        for i in range(n_in - 1):
            y_cp[f * (n_in - 1) + i].wait_recv()
            pair = pair + yr[i, f].astype(F32)
        hp[f] = pair
        zb[f] = pair.astype(BF16)
        for i, p in enumerate(out_peers):
            z_cp.append(
                send(zb.at[f, p], zr.at[i, f], z_ss.at[i, f], z_rs.at[i, f],
                     {"vocab": p * n_in + inner})
            )
        if f == f_chunks // 2:
            head_acc[...] = jnp.dot(hown[...], grad[...], preferred_element_type=F32)

    head = head_acc[...]
    numerator = num[...]
    for i in range(n_tok - 1):
        h_cp[i].wait_recv()
        n_cp[i].wait_recv()
        numerator = numerator + nrecv[i]
        theirs = hrecv[i].T
        g_cp[i].wait_recv()
        head = head + jnp.dot(theirs, grecv[i], preferred_element_type=F32)
    head_ref[...] = head.astype(BF16)
    loss_ref[...] = numerator / live_total

    for f in range(f_chunks):
        hid = hp[f, outer]
        for i in range(n_out - 1):
            z_cp[f * (n_out - 1) + i].wait_recv()
            hid = hid + zr[i, f].astype(F32)
        hid_ref[:, f * fw:(f + 1) * fw] = hid.astype(BF16)
    for copy in p_cp + c_cp + h_cp + s_cp + g_cp + n_cp + y_cp + z_cp:
        copy.wait_send()


def emit(loss_in, head_in, hid_in, loss_out, head_out, hid_out, sems):
    piece = head_in.shape[0] // 4
    copies = [pltpu.make_async_copy(hid_in, hid_out, sems.at[4])] + [
        pltpu.make_async_copy(
            head_in.at[pl.ds(i * piece, piece)], head_out.at[pl.ds(i * piece, piece)], sems.at[i]
        )
        for i in range(4)
    ]
    for copy in copies:
        copy.start()
    loss_out[...] = loss_in[0:1, 0:1]
    for copy in copies:
        copy.wait()


def fused_body(n_tok, n_voc, teacher_hidden, teacher_head, student_hidden, student_head, live_counts):
    rows, t_feats = teacher_hidden.shape
    feats, width = student_head.shape
    cw, fw = width // 2, feats // 6
    block, out_rows = feats // n_tok, rows // n_voc
    n_in, n_out = 2, n_voc // 2
    tp, vp, ip, op, nf = n_tok - 1, n_voc - 1, n_in - 1, n_out - 1, feats // fw
    vmem, dma = pltpu.VMEM, pltpu.SemaphoreType.DMA
    any_spec = pl.BlockSpec(memory_space=pl.ANY)
    vm_spec = pl.BlockSpec(memory_space=pltpu.VMEM)
    loss, head, hid = pl.pallas_call(
        functools.partial(fused, n_tok, n_in, n_out, cw, fw),
        out_shape=(
            jax.ShapeDtypeStruct((8, 128), F32),
            jax.ShapeDtypeStruct((block, width), BF16),
            jax.ShapeDtypeStruct((out_rows, feats), BF16),
        ),
        in_specs=[pl.BlockSpec(memory_space=pltpu.SMEM)] + [any_spec] * 4,
        out_specs=(vm_spec,) * 3,
        scratch_shapes=[
            vmem((rows, t_feats), BF16), vmem((2, t_feats, cw), BF16),
            vmem((rows, feats), BF16), vmem((feats, width), BF16),
            vmem((4, rows, cw), F32), vmem((4, rows, cw), F32),
            vmem((2, rows, cw), F32), vmem((2, rows, cw), F32),
            vmem((rows, 128), F32), vmem((8, rows), F32), vmem((vp, 8, rows), F32),
            vmem((8, 128), F32), vmem((tp, 8, 128), F32),
            vmem((8, 128), F32), vmem((tp, 8, 128), F32),
            vmem((block, rows), BF16), vmem((tp, rows, block), BF16),
            vmem((rows, width), BF16), vmem((tp, rows, width), BF16),
            vmem((block, width), F32),
            vmem((nf, n_out, n_in, out_rows, fw), F32), vmem((nf, n_out, n_in, out_rows, fw), BF16),
            vmem((ip, nf, n_out, out_rows, fw), BF16),
            vmem((nf, n_out, out_rows, fw), F32), vmem((nf, n_out, out_rows, fw), BF16),
            vmem((op, nf, out_rows, fw), BF16),
            dma((5,)), dma((4,)), dma((4,)), dma((tp,)), dma((tp,)), dma((tp,)), dma((tp,)),
            dma((vp,)), dma((vp,)), dma((tp,)), dma((tp,)), dma((tp,)), dma((tp,)),
            dma((ip, nf)), dma((ip, nf)), dma((op, nf)), dma((op, nf)),
        ],
        compiler_params=pltpu.CompilerParams(
            collective_id=0, has_side_effects=True, vmem_limit_bytes=53 * 1024 * 1024
        ),
    )(live_counts, teacher_hidden, teacher_head, student_hidden, student_head)
    loss, head, hid = pl.pallas_call(
        emit,
        out_shape=(
            jax.ShapeDtypeStruct((1, 1), F32),
            jax.ShapeDtypeStruct(head.shape, BF16),
            jax.ShapeDtypeStruct(hid.shape, BF16),
        ),
        in_specs=[vm_spec, any_spec, any_spec],
        out_specs=(vm_spec, any_spec, any_spec),
        scratch_shapes=[dma((5,))],
        compiler_params=pltpu.CompilerParams(vmem_limit_bytes=4 * 1024 * 1024),
    )(loss, head, hid)
    return (loss[0, 0], head, hid)


def solution(mesh):
    placed = (P("tok", "sect"), P("sect", "vocab"), P("tok", "sect"), P("sect", "vocab"), P("tok"))
    n_tok, n_voc = mesh.shape["tok"], mesh.shape["vocab"]

    def run(*args):
        rows = args[0].shape[0]
        if rows % (TILE * n_voc) == 0 and n_voc % 2 == 0 and n_voc > 2 and n_tok > 1:
            return fused_body(n_tok, n_voc, *args)
        return body(*args)

    return jax.shard_map(
        run,
        mesh=mesh,
        in_specs=placed,
        out_specs=(P(), P(("sect", "tok"), "vocab"), P(("tok", "vocab"), "sect")),
        check_vma=False,
    )
```
